32 devices in a mesh: group: 2 (over x), dp: 16 (over z, y, core).
Axes of the slice: x: 2, y: 2, z: 4, core: 2. Of those that a mesh axis runs over, the one named last changes fastest.
Arguments:
- tokens: bfloat16 [512, 4096], P(('group', 'dp')), parts along dimension 0, may hold values from -6 to 6
- cotangent: bfloat16 [512, 8192], P('group', 'dp'), parts along dimension 0, may hold values from -0.75 to 0.75
- token_weight: float32 [512], P('group'), parts along dimension 0, may hold values from 0.5 to 1.5
- weight: bfloat16 [4096, 8192], P(None, 'dp'), may hold values from -0.09375 to 0.09375
- moment_one: bfloat16 [4096, 8192], P(None, 'dp'), may hold values from -6 to 6
- moment_two: bfloat16 [4096, 8192], P(None, 'dp'), may hold values from 0.003 to 10
- adjoint: float32 [4096, 8192], P(None, 'dp'), may hold values from -5 to 5
Outputs:
- theta_bar: float32 [8192, 8192], P('group', 'dp'), parts along dimension 0
- token_scores: float32 [512], P(('group', 'dp')), parts along dimension 0
The draws below stay inside these ranges and needn't reach their ends.
There are 2 independent parts, one for each index of `group`. The reference program is written for one: setup_inputs(seed, part) draws one part's arguments, and reference() takes and returns one part's arrays. A program takes and returns all parts, laid end to end along the dimension named above; an argument that names none is the same for every part. Nothing has to cross between parts.
All inputs are finite; a program needn't handle non-finite values.
Results may differ from the reference program's by a relative error of at most 0.0038.
Values may be sent and summed in bfloat16 or wider, within the bound.
A program may use at most 128 MiB of HBM per device.

```python
import math
import jax
import jax.numpy as jnp
from jax import lax

D = 4096
FW = 8192
TOKENS = 256


def moment_fields(key):
    key = jax.random.fold_in(key, 7)
    key_one, key_rows, key_cols, key_base = jax.random.split(key, 4)
    ln_ten = math.log(10.0)
    one = jax.random.truncated_normal(key_one, -6.0, 6.0, (D, FW), jnp.float32)
    rows = jnp.exp(jax.random.uniform(key_rows, (D, 1), jnp.float32) * ln_ten)
    cols = jnp.exp(jax.random.uniform(key_cols, (1, FW), jnp.float32) * ln_ten)
    base = jnp.exp(jax.random.uniform(key_base, (D, FW), jnp.float32, -1.2, 1.2))
    place = jnp.arange(FW, dtype=jnp.float32)[None, :] / (FW - 1)
    trend = jnp.exp(-math.log(3.0) * place)
    two = 0.03 * base * rows * cols * trend
    return (one, two)


def draw_moment_one(key, part):
    one, two = moment_fields(key)
    return one.astype(jnp.bfloat16)


def draw_moment_two(key, part):
    one, two = moment_fields(key)
    return two.astype(jnp.bfloat16)


def draw_adjoint(key, part):
    one, two = moment_fields(key)
    ratio = one / jnp.sqrt(two + 0.05)
    noise_key = jax.random.fold_in(key, 11)
    along = 1.5 * jnp.tanh(ratio / 3.0)
    noise = 0.8 * jax.random.truncated_normal(noise_key, -4.0, 4.0, (D, FW), jnp.float32)
    return along + noise


def levels(rng, dims, cuts, least, high):
    def one(position, blocks):
        steps = jax.random.uniform(jax.random.fold_in(jax.random.fold_in(rng, 6), position), (blocks,), jnp.float32, least / len(cuts), high / len(cuts))
        return jnp.repeat(jnp.exp(steps), dims[position] // blocks).reshape((-1,) + (1,) * (len(dims) - position - 1))

    factor_of = one(*cuts[0])
    for cut in cuts[1:]:
        factor_of = factor_of * one(*cut)
    return factor_of


def normal_values(key, dims, scale, reach, shards=(), held_as=jnp.bfloat16):
    loudness = levels(key, dims, shards, -0.22, 0.18) if shards else 1.0
    result = jax.random.normal(key, dims, jnp.float32) * scale * loudness
    return jnp.minimum(jnp.maximum(result, -reach), reach).astype(held_as)


def setup_inputs(seed: int = 0, part: int = 0) -> dict:
    seeds = jax.random.split(jax.random.key(seed), 8)
    own_keys = jax.random.split(jax.random.fold_in(seeds[7], part), 8)
    return {
        "tokens": normal_values(own_keys[0], (TOKENS, D), 1.0, 6.0, ((0, 16),)),
        "cotangent": normal_values(own_keys[1], (TOKENS, FW), 0.05, 0.75, ((1, 16),)),
        "token_weight": jnp.clip(jax.random.uniform(own_keys[2], (TOKENS,), jnp.float32, 0.5, 1.5), 0.5, 1.5),
        "weight": normal_values(seeds[3], (D, FW), D ** -0.5, 0.09375, ((1, 16),)),
        "moment_one": draw_moment_one(jax.random.fold_in(seeds[7], 71), part),
        "moment_two": draw_moment_two(jax.random.fold_in(seeds[7], 71), part),
        "adjoint": draw_adjoint(jax.random.fold_in(seeds[7], 71), part),
    }


def slopes(gate):
    sig = jax.nn.sigmoid(gate)
    slope = sig * (1.0 + gate * (1.0 - sig))
    curve = sig * (1.0 - sig) * (2.0 + gate * (1.0 - 2.0 * sig))
    return (slope, curve)

def reference(tokens, cotangent, token_weight, weight, moment_one, moment_two, adjoint):
    gate = jnp.dot(tokens, weight, preferred_element_type=jnp.float32)
    slope, curve = slopes(gate)
    cot_f = cotangent.astype(jnp.float32)
    scaled = (token_weight[:, None] * cot_f * slope).astype(jnp.bfloat16)
    grad = lax.dot_general(tokens, scaled, (((0,), (0,)), ((), ())), preferred_element_type=jnp.float32)
    first = 0.9 * moment_one.astype(jnp.float32) + 0.1 * grad
    second = 0.95 * moment_two.astype(jnp.float32) + 0.05 * grad * grad
    root = jnp.sqrt(second)
    den = root + 1e-08
    upd = first / den
    count = D * FW
    sq = jnp.sum(upd * upd)
    cross = jnp.sum(adjoint * upd)
    rms = jnp.sqrt(sq / count)
    scale = 1.0 / jnp.maximum(1.0, rms)
    bind = jnp.where(rms > 1.0, 1.0 / (rms * rms * rms), 0.0)
    ubar = -0.01 * scale * adjoint + 0.01 * cross * bind / count * upd
    mbar = ubar / den
    vbar = -ubar * first / (den * den) / (2.0 * root)
    gbar = (0.1 * mbar + 0.1 * grad * vbar).astype(jnp.bfloat16)
    probe = jnp.dot(tokens, gbar, preferred_element_type=jnp.float32)
    bent = (token_weight[:, None] * cot_f * curve * probe).astype(jnp.bfloat16)
    theta_bar = 0.999 * adjoint + lax.dot_general(tokens, bent, (((0,), (0,)), ((), ())), preferred_element_type=jnp.float32)
    token_scores = lax.optimization_barrier(jnp.sum(cot_f * slope * probe, axis=1))
    return (theta_bar, token_scores)
```

```python
import functools
import math

import jax
import jax.numpy as jnp
from jax import lax
from jax.experimental import pallas as pl
from jax.experimental.pallas import tpu as pltpu
from jax.sharding import PartitionSpec as P

D = 4096
FW = 8192
COUNT = D * FW
MESH = pl.DeviceIdType.MESH
KB = 512
STRIP = 16
LAST = 16
EPS = math.sqrt(20.0) * 1e-08


def dot(a, b):
    return jnp.dot(a, b, preferred_element_type=jnp.float32)


def dot_rows(a, b):
    return lax.dot_general(a, b, (((0,), (0,)), ((), ())), preferred_element_type=jnp.float32)


def main_kernel(
    n, wide, pieces,
    x_hbm, cot_hbm, tw_hbm, w_hbm, one_hbm, two_hbm, adj_hbm,
    tok, adj, bent_out, score_out,
    x, cot, tw_s, w, one, two, gate_s, p_s, q_s, scaled_s, g_even, g_odd,
    a_even, a_odd, b_even, b_odd, pa, pb, mine, inbox,
    load_sem, own_sem, gs, gr, ss, sr,
):
    me = lax.axis_index("dp")
    line = n // (2 * wide)
    core = lax.rem(me, 2)
    y = lax.rem(me // 2, wide)
    z = me // (2 * wide)
    stride = 2 * wide
    sibling = me + 1 - 2 * core
    across = me + (1 - 2 * y) * 2
    rows = x.shape[0]
    tokens, width = scaled_s.shape
    cols = D // pieces
    more, less = z + 1 < line, z > 0

    loads = [
        pltpu.make_async_copy(src, dst, load_sem.at[i])
        for i, (src, dst) in enumerate(
            ((cot_hbm, cot), (tw_hbm, tw_s), (w_hbm, w), (two_hbm, two), (one_hbm, one), (adj_hbm, adj)))
    ]
    own = [
        pltpu.make_async_copy(x_hbm, x, own_sem.at[0]),
        pltpu.make_async_copy(x_hbm, tok.at[pl.ds(pl.multiple_of(me * rows, rows), rows), :], own_sem.at[1]),
    ]

    def slab(o, h):
        return tok.at[pl.ds(pl.multiple_of(o * rows, rows), rows), pl.ds(h * cols, cols)]

    barrier = pltpu.get_barrier_semaphore()

    def greet(dev):
        pl.semaphore_signal(barrier, inc=1, device_id={"dp": dev}, device_id_type=MESH)

    greet(sibling)
    if wide == 2:
        greet(across)

    @pl.when(more)
    def _():
        greet(me + stride)

    @pl.when(less)
    def _():
        greet(me - stride)

    for copy in own + loads:
        copy.start()
    own[0].wait()
    pl.semaphore_wait(barrier, wide + more.astype(jnp.int32) + less.astype(jnp.int32))

    def push(kind, o, dev, h, src=None):
        return pltpu.make_async_remote_copy(
            src_ref=slab(o, h) if src is None else src.at[:, pl.ds(h * cols, cols)],
            dst_ref=slab(o, h),
            send_sem=gs.at[kind, h, o],
            recv_sem=gr.at[h, o],
            device_id={"dp": dev},
            device_id_type=MESH,
        )

    def arrive(o, h):
        push(3, o, sibling, h).wait_recv()

    for h in range(pieces):
        @pl.when(more)
        def _():
            push(0, me, me + stride, h, x).start()

        @pl.when(less)
        def _():
            push(1, me, me - stride, h, x).start()

        if wide == 2:
            push(2, me, across, h, x).start()
        push(3, me, sibling, h, x).start()

    def from_across(k, h):
        if wide != 2:
            return
        for way in (-1, 1) if k else (1,):
            o = across + way * k * stride

            @pl.when((z + way * k >= 0) & (z + way * k < line))
            def _():
                arrive(o, h)
                push(3, o, sibling, h).start()

    for k in range(1, line):
        for h in range(pieces):
            for way, kind, onward in ((-1, 0, more), (1, 1, less)):
                o = me + way * k * stride

                @pl.when((z + way * k >= 0) & (z + way * k < line))
                def _():
                    arrive(o, h)

                    @pl.when(onward)
                    def _():
                        push(kind, o, me - way * stride, h).start()

                    if wide == 2:
                        push(2, o, across, h).start()
                    push(3, o, sibling, h).start()

            from_across(k - 1, h)
    for h in range(pieces):
        from_across(line - 1, h)

    def from_sibling(i, _):
        for h in range(pieces):
            arrive(2 * i + 1 - core, h)
        return 0

    lax.fori_loop(0, n // 2, from_sibling, 0)
    own[1].wait()
    for copy in loads[:3]:
        copy.wait()
    gate_s[...] = jnp.zeros_like(gate_s)

    def gate_step(i, _):
        ks = pl.ds(pl.multiple_of(i * 1024, 1024), 1024)
        gate_s[...] += dot(tok[:, ks], w[ks, :])
        return 0

    lax.fori_loop(0, D // 1024, gate_step, 0)

    tw = jnp.transpose(jnp.broadcast_to(tw_s[...], (128, tokens)))
    q_s[:, 0:128] = tw

    def slope_step(i, _):
        rs = pl.ds(pl.multiple_of(i * STRIP, STRIP), STRIP)
        tw = q_s[rs, 0:128]
        for j in range(width // 128):
            js = slice(j * 128, (j + 1) * 128)
            gate = gate_s[rs, js]
            cot_f = cot[rs, js].astype(jnp.float32)
            sig = jax.nn.sigmoid(gate)
            slope = sig * (1.0 + gate * (1.0 - sig))
            curve = sig * (1.0 - sig) * (2.0 + gate * (1.0 - 2.0 * sig))
            scaled_s[rs, js] = (tw * cot_f * slope).astype(jnp.bfloat16)
            p_s[rs, js] = cot_f * slope
            q_s[rs, js] = tw * cot_f * curve
        return 0

    lax.fori_loop(0, tokens // STRIP, slope_step, 0, unroll=4)

    for copy in loads[3:]:
        copy.wait()

    def fold(v):
        out = None
        for i in range(v.shape[0] // 8):
            for j in range(width // 128):
                part = v[i * 8:(i + 1) * 8, j * 128:(j + 1) * 128]
                out = part if out is None else out + part
        return out

    def fields(rs, g):
        second = 19.0 * two[rs, :].astype(jnp.float32) + g * g
        inv_root = lax.rsqrt(second)
        den = second * inv_root + EPS
        inv = lax.rsqrt(den * den)
        upd = (9.0 * one[rs, :].astype(jnp.float32) + g) * inv
        return inv_root, inv, upd

    def columns(i):
        return pl.ds(pl.multiple_of(i * KB, KB), KB)

    def strip(i, r):
        return pl.ds(pl.multiple_of(i * KB + r, STRIP), STRIP)

    def grad(i, out):
        out[...] = dot_rows(tok[:, columns(i)], scaled_s[...])

    grad(0, g_even)
    sq = cross = jnp.zeros((8, 128), jnp.float32)
    for r in range(0, KB, KB // 4):
        _, _, upd = fields(strip(0, r), g_even[r:r + STRIP, :])
        sq = sq + fold(upd * upd)
        cross = cross + fold(adj[strip(0, r), :] * upd)
    share = jnp.sum(cross, keepdims=True) / (jnp.sum(sq, keepdims=True) + 1e-03)
    share_s = jnp.broadcast_to(share, (STRIP, width))

    pa[...] = jnp.zeros_like(pa)
    pb[...] = jnp.zeros_like(pb)

    def half(i, g_now, g_next, a_now, b_now, a_last, b_last, carry, first):
        sq, cross = carry
        grad(jnp.minimum(i + 1, D // KB - 1), g_next)
        for r in range(0, KB, STRIP):
            rs = strip(i, r)
            g = g_now[r:r + STRIP, :]
            inv_root, inv, upd = fields(rs, g)
            slope = inv - inv * ((g * inv_root) * upd)
            adj_r = adj[rs, :]
            sq = sq + fold(upd * upd)
            cross = cross + fold(adj_r * upd)
            a_now[r:r + STRIP, :] = ((adj_r - share_s * upd) * slope).astype(jnp.bfloat16)
            b_now[r:r + STRIP, :] = (upd * slope).astype(jnp.bfloat16)
        left = tok[:, columns(jnp.maximum(i - 1, 0))]
        pa[...] += dot(left, a_last[...])
        pb[...] += dot(left, b_last[...])
        return sq, cross

    a_odd[...] = jnp.zeros_like(a_odd)
    b_odd[...] = jnp.zeros_like(b_odd)

    def both(j, carry):
        carry = half(2 * j, g_even, g_odd, a_even, b_even, a_odd, b_odd, carry, True)
        return half(2 * j + 1, g_odd, g_even, a_odd, b_odd, a_even, b_even, carry, False)

    zero = jnp.zeros((8, 128), jnp.float32)
    sq, cross = lax.fori_loop(0, D // KB // 2, both, (zero, zero))
    left = tok[:, D - KB:]
    pb[...] += dot(left, b_odd[...])
    pa[...] += dot(left, a_odd[...]) + share * pb[...]

    pair = jnp.concatenate(
        [jnp.sum(sq, axis=0, keepdims=True), jnp.sum(cross, axis=0, keepdims=True)], axis=0)
    at = lax.broadcasted_iota(jnp.int32, (rows, 128), 0)
    lane = lax.broadcasted_iota(jnp.int32, (rows, 128), 1)

    def score_step(i, _):
        rs = pl.ds(pl.multiple_of(i * rows, rows), rows)
        out = []
        for ref in (pa, pb):
            part = fold_lanes(p_s[rs, :] * ref[rs, :])
            total = jnp.sum(part, axis=1, keepdims=True)
            out.append(jnp.sum(jnp.where(at == lane, total, 0.0), axis=0, keepdims=True))
        mine[i] = jnp.concatenate(out + [pair], axis=0)
        return 0

    def fold_lanes(v):
        out = v[:, 0:128]
        for j in range(1, width // 128):
            out = out + v[:, j * 128:(j + 1) * 128]
        return out

    lax.fori_loop(0, n, score_step, 0, unroll=4)

    def each(body):
        def step(k, _):
            body(k)
            return 0

        lax.fori_loop(1, n, step, 0)

    def send(k):
        o = lax.rem(me + k, n)
        return pltpu.make_async_remote_copy(
            src_ref=mine.at[o], dst_ref=inbox.at[me],
            send_sem=ss.at[k], recv_sem=sr.at[me],
            device_id={"dp": o}, device_id_type=MESH)

    def receive(k):
        o = lax.rem(me + k, n)
        pltpu.make_async_remote_copy(
            src_ref=mine.at[o], dst_ref=inbox.at[o],
            send_sem=ss.at[k], recv_sem=sr.at[o],
            device_id={"dp": o}, device_id_type=MESH).wait_recv()

    each(lambda k: send(k).start())
    inbox[me] = mine[me]

    def bent_step(i, _):
        rs = pl.ds(pl.multiple_of(i * STRIP, STRIP), STRIP)
        pa[rs, :] = q_s[rs, :] * pa[rs, :]
        pb[rs, :] = q_s[rs, :] * pb[rs, :]
        return 0

    lax.fori_loop(0, tokens // STRIP, bent_step, 0, unroll=4)

    def sent_line(i, _):
        o = (i * wide + y) * 2 + core
        for h in range(pieces):
            @pl.when((i <= z) & more)
            def _():
                push(0, o, me + stride, h).wait_send()

            @pl.when((i >= z) & less)
            def _():
                push(1, o, me - stride, h).wait_send()

            if wide == 2:
                push(2, o, across, h).wait_send()
        return 0

    lax.fori_loop(0, line, sent_line, 0)

    def sent_core(i, _):
        for h in range(pieces):
            push(3, 2 * i + core, sibling, h).wait_send()
        return 0

    lax.fori_loop(0, n // 2, sent_core, 0)
    each(receive)

    tot = inbox[0]
    for o in range(1, n):
        tot = tot + inbox[o]
    sq = 0.2 * jnp.sum(tot[2:3], keepdims=True)
    cross = math.sqrt(0.2) * jnp.sum(tot[3:4], keepdims=True)
    rms = jnp.sqrt(sq / COUNT)
    scale = 1.0 / jnp.maximum(1.0, rms)
    bind = jnp.where(rms > 1.0, 1.0 / (rms * rms * rms), 0.0)
    alpha = (-0.01 * 0.1 * math.sqrt(20.0)) * scale
    beta = (0.01 * 0.2) * cross * bind / COUNT
    score_out[...] = alpha * tot[0:1] + beta * tot[1:2]
    alpha = jnp.broadcast_to(alpha, (STRIP, width))
    beta = jnp.broadcast_to(beta, (STRIP, width))

    def last_step(i, _):
        rs = pl.ds(pl.multiple_of(i * STRIP, STRIP), STRIP)
        bent_out[rs, :] = (alpha * pa[rs, :] + beta * pb[rs, :]).astype(jnp.bfloat16)
        return 0

    lax.fori_loop(0, tokens // STRIP, last_step, 0, unroll=4)
    each(lambda k: send(k).wait_send())


def last_kernel(tok, bent, adj, sc, theta_hbm, score, theta, out_sem):
    step = D // LAST
    parts = [pl.ds(i * step, step) for i in range(LAST)]
    outs = [pltpu.make_async_copy(theta.at[p, :], theta_hbm.at[p, :], out_sem.at[i]) for i, p in enumerate(parts)]
    for i, p in enumerate(parts):
        theta[p, :] = 0.999 * adj[p, :] + dot_rows(tok[:, p], bent[...])
        outs[i].start()
    score[...] = sc[:, :score.shape[1]]
    for copy in outs:
        copy.wait()


def shards(n, wide, x, cotangent, token_weight, weight, moment_one, moment_two, adjoint):
    rows = x.shape[0]
    tokens = n * rows
    width = weight.shape[1]
    pieces = 4 if n <= 16 else 1
    f32, bf16 = jnp.float32, jnp.bfloat16
    vm = pl.BlockSpec(memory_space=pltpu.VMEM)
    hbm = pl.BlockSpec(memory_space=pltpu.HBM)
    dma = pltpu.SemaphoreType.DMA
    tok, adj, bent, sc = pl.pallas_call(
        functools.partial(main_kernel, n, wide, pieces),
        out_shape=(
            pltpu.VMEM((tokens, D), bf16),
            pltpu.VMEM((D, width), f32),
            pltpu.VMEM((tokens, width), bf16),
            pltpu.VMEM((1, 128), f32),
        ),
        in_specs=[hbm] * 7,
        out_specs=(vm, vm, vm, vm),
        scratch_shapes=[
            pltpu.VMEM((rows, D), bf16),
            pltpu.VMEM((tokens, width), bf16),
            pltpu.VMEM((1, tokens), f32),
            pltpu.VMEM((D, width), bf16),
            pltpu.VMEM((D, width), bf16),
            pltpu.VMEM((D, width), bf16),
            pltpu.VMEM((tokens, width), f32),
            pltpu.VMEM((tokens, width), f32),
            pltpu.VMEM((tokens, width), f32),
            pltpu.VMEM((tokens, width), bf16),
            pltpu.VMEM((KB, width), f32),
            pltpu.VMEM((KB, width), f32),
            pltpu.VMEM((KB, width), bf16),
            pltpu.VMEM((KB, width), bf16),
            pltpu.VMEM((KB, width), bf16),
            pltpu.VMEM((KB, width), bf16),
            pltpu.VMEM((tokens, width), f32),
            pltpu.VMEM((tokens, width), f32),
            pltpu.VMEM((n, 4, 128), f32),
            pltpu.VMEM((n, 4, 128), f32),
            dma((6,)),
            dma((2,)),
            dma((4, pieces, n)),
            dma((pieces, n)),
            dma((n,)),
            dma((n,)),
        ],
        compiler_params=pltpu.CompilerParams(
            collective_id=0, has_side_effects=True, vmem_limit_bytes=36 * 2**20
        ),
    )(*(
        pltpu.with_memory_space_constraint(a, pltpu.HBM)
        for a in (x, cotangent, token_weight.reshape(1, tokens), weight, moment_one, moment_two, adjoint)
    ))
    theta, score = pl.pallas_call(
        last_kernel,
        out_shape=(
            jax.ShapeDtypeStruct((D, width), f32),
            jax.ShapeDtypeStruct((1, rows), f32),
        ),
        in_specs=[vm] * 4,
        out_specs=(hbm, vm),
        scratch_shapes=[pltpu.VMEM((D, width), f32), dma((LAST,))],
        compiler_params=pltpu.CompilerParams(vmem_limit_bytes=36 * 2**20),
    )(tok, bent, adj, sc)
    return theta, score.reshape(rows)


def solution(mesh):
    n = mesh.shape["dp"]
    wide = 2 if mesh.shape["group"] == 2 else 1
    in_specs = (
        P(("group", "dp"), None),
        P("group", "dp"),
        P("group"),
        P(None, "dp"),
        P(None, "dp"),
        P(None, "dp"),
        P(None, "dp"),
    )
    out_specs = (P("group", "dp"), P(("group", "dp")))
    return jax.shard_map(
        functools.partial(shards, n, wide), mesh=mesh,
        in_specs=in_specs, out_specs=out_specs, check_vma=False)
```

```python
import functools
import math

import jax
import jax.numpy as jnp
from jax import lax
from jax.experimental import pallas as pl
from jax.experimental.pallas import tpu as pltpu
from jax.sharding import PartitionSpec as P

D = 4096
FW = 8192
COUNT = D * FW
MESH = pl.DeviceIdType.MESH
KB = 2048
STRIP = 16
LAST = 16
EPS = math.sqrt(20.0) * 1e-08


def dot(a, b):
    return jnp.dot(a, b, preferred_element_type=jnp.float32)


def dot_rows(a, b):
    return lax.dot_general(a, b, (((0,), (0,)), ((), ())), preferred_element_type=jnp.float32)


def main_kernel(
    n, wide, pieces,
    x_hbm, cot_hbm, tw_hbm, w_hbm, one_hbm, two_hbm, adj_hbm,
    tok, adj, bent_out, score_out,
    cot, tw_s, w, one, two, gate_s, p_s, q_s, scaled_s, g_even,
    a_even, b_even, pa, pb, mine, inbox,
    load_sem, block_sem, own_sem, zs, zr, ys, yr, cs, cr, ss, sr,
):
    me = lax.axis_index("dp")
    line = n // (2 * wide)
    core = lax.rem(me, 2)
    y = lax.rem(me // 2, wide)
    z = me // (2 * wide)
    stride = 2 * wide
    sibling = me + 1 - 2 * core
    across = me + (1 - 2 * y) * 2
    rows = x_hbm.shape[0]
    tokens, width = scaled_s.shape
    cols = D // pieces
    more, less = z + 1 < line, z > 0

    first_loads = [
        pltpu.make_async_copy(src, dst, load_sem.at[i])
        for i, (src, dst) in enumerate(((w_hbm, w), (cot_hbm, cot), (tw_hbm, tw_s)))
    ]

    def block_loads(i):
        p = pl.ds(pl.multiple_of(i * KB, KB), KB)
        return [
            pltpu.make_async_copy(src.at[p, :], dst.at[p, :], block_sem.at[j, i])
            for j, (src, dst) in enumerate(((two_hbm, two), (one_hbm, one), (adj_hbm, adj)))
        ]

    def slab(o):
        return tok.at[pl.ds(pl.multiple_of(o * rows, rows), rows), :]

    def piece(ref, h):
        return ref.at[:, pl.ds(h * cols, cols)]

    own = pltpu.make_async_copy(x_hbm, slab(me), own_sem)

    barrier = pltpu.get_barrier_semaphore()

    def greet(dev):
        pl.semaphore_signal(barrier, inc=1, device_id={"dp": dev}, device_id_type=MESH)

    greet(sibling)
    if wide == 2:
        greet(across)

    @pl.when(more)
    def _():
        greet(me + stride)

    @pl.when(less)
    def _():
        greet(me - stride)

    own.start()
    pl.semaphore_wait(barrier, wide + more.astype(jnp.int32) + less.astype(jnp.int32))

    def along(up, o, h, src=None):
        return pltpu.make_async_remote_copy(
            src_ref=piece(slab(o) if src is None else src, h), dst_ref=piece(slab(o), h),
            send_sem=zs.at[0 if up else 1, o], recv_sem=zr.at[h, o],
            device_id={"dp": me + stride if up else me - stride}, device_id_type=MESH)

    def over(o, h=None, src=None):
        src = slab(o) if src is None else src
        return pltpu.make_async_remote_copy(
            src_ref=src if h is None else piece(src, h), dst_ref=slab(o) if h is None else piece(slab(o), h),
            send_sem=ys.at[o], recv_sem=yr.at[o],
            device_id={"dp": across}, device_id_type=MESH)

    def beside(o, src=None):
        return pltpu.make_async_remote_copy(
            src_ref=slab(o) if src is None else src, dst_ref=slab(o),
            send_sem=cs, recv_sem=cr,
            device_id={"dp": sibling}, device_id_type=MESH)

    def beside_all():
        half = tok.at[pl.ds(0, tokens // 2), :]
        return pltpu.make_async_remote_copy(
            src_ref=half, dst_ref=half, send_sem=cs, recv_sem=cr,
            device_id={"dp": sibling}, device_id_type=MESH)

    for h in range(pieces):
        @pl.when(more)
        def _():
            along(True, me, h, x_hbm).start()

        @pl.when(less)
        def _():
            along(False, me, h, x_hbm).start()

        if wide == 2:
            over(me, h, x_hbm).start()
    beside(me, x_hbm).start()
    for copy in first_loads:
        copy.start()

    def from_across(k):
        if wide != 2:
            return
        for way in (-1, 1) if k else (1,):
            o = across + way * k * stride

            @pl.when((z + way * k >= 0) & (z + way * k < line))
            def _():
                over(o).wait_recv()
                beside(o).start()

    for k in range(1, line):
        for h in range(pieces):
            for way, onward in ((-1, more), (1, less)):
                o = me + way * k * stride

                @pl.when((z + way * k >= 0) & (z + way * k < line))
                def _():
                    along(way < 0, o, h).wait_recv()

                    @pl.when(onward)
                    def _():
                        along(way < 0, o, h).start()

                    if wide == 2:
                        over(o, h).start()
                    if h == pieces - 1:
                        beside(o).start()

        from_across(k - 1)
    for i in range(D // KB):
        for copy in block_loads(i):
            copy.start()
    from_across(line - 1)
    beside_all().wait_recv()
    own.wait()
    for copy in first_loads:
        copy.wait()
    gate_s[...] = jnp.zeros_like(gate_s)

    def gate_step(i, _):
        ks = pl.ds(pl.multiple_of(i * 1024, 1024), 1024)
        gate_s[...] += dot(tok[:, ks], w[ks, :])
        return 0

    lax.fori_loop(0, D // 1024, gate_step, 0)

    tw = jnp.transpose(jnp.broadcast_to(tw_s[...], (128, tokens)))
    q_s[:, 0:128] = tw

    def slope_step(i, _):
        rs = pl.ds(pl.multiple_of(i * STRIP, STRIP), STRIP)
        tw = q_s[rs, 0:128]
        for j in range(width // 128):
            js = slice(j * 128, (j + 1) * 128)
            gate = gate_s[rs, js]
            cot_f = cot[rs, js].astype(jnp.float32)
            sig = jax.nn.sigmoid(gate)
            slope = sig * (1.0 + gate * (1.0 - sig))
            curve = sig * (1.0 - sig) * (2.0 + gate * (1.0 - 2.0 * sig))
            scaled_s[rs, js] = (tw * cot_f * slope).astype(jnp.bfloat16)
            p_s[rs, js] = cot_f * slope
            q_s[rs, js] = tw * cot_f * curve
        return 0

    lax.fori_loop(0, tokens // STRIP, slope_step, 0, unroll=4)

    def fold(v):
        out = None
        for i in range(v.shape[0] // 8):
            for j in range(width // 128):
                part = v[i * 8:(i + 1) * 8, j * 128:(j + 1) * 128]
                out = part if out is None else out + part
        return out

    def fields(rs, g):
        second = 19.0 * two[rs, :].astype(jnp.float32) + g * g
        inv_root = lax.rsqrt(second)
        den = second * inv_root + EPS
        inv = lax.rsqrt(den * den)
        upd = (9.0 * one[rs, :].astype(jnp.float32) + g) * inv
        return inv_root, inv, upd

    def columns(i):
        return pl.ds(pl.multiple_of(i * KB, KB), KB)

    def strip(i, r):
        return pl.ds(pl.multiple_of(i * KB + r, STRIP), STRIP)

    def grad(i, out):
        out[...] = dot_rows(tok[:, columns(i)], scaled_s[...])

    grad(0, g_even)
    for copy in block_loads(0):
        copy.wait()
    sq = cross = jnp.zeros((8, 128), jnp.float32)
    for r in range(0, KB, KB // 4):
        _, _, upd = fields(strip(0, r), g_even[r:r + STRIP, :])
        sq = sq + fold(upd * upd)
        cross = cross + fold(adj[strip(0, r), :] * upd)
    share = jnp.sum(cross, keepdims=True) / (jnp.sum(sq, keepdims=True) + 1e-03)

    pa[...] = jnp.zeros_like(pa)
    pb[...] = jnp.zeros_like(pb)

    def block(i, carry):
        base = i * KB

        @pl.when(i > 0)
        def _():
            grad(i, g_even)
            for copy in block_loads(i):
                copy.wait()

        def fill(r, carry):
            sq, cross = carry
            here = pl.ds(pl.multiple_of(r * 16, 16), 16)
            rs = pl.ds(pl.multiple_of(base + r * 16, 16), 16)
            g = g_even[here, :]
            inv_root, inv, upd = fields(rs, g)
            slope = inv - inv * ((g * inv_root) * upd)
            adj_r = adj[rs, :]
            sq = sq + fold(upd * upd)
            cross = cross + fold(adj_r * upd)
            a_even[here, :] = ((adj_r - share * upd) * slope).astype(jnp.bfloat16)
            b_even[here, :] = (upd * slope).astype(jnp.bfloat16)
            return sq, cross

        carry = lax.fori_loop(0, KB // 16, fill, carry, unroll=4)
        left = tok[:, columns(i)]
        pa[...] += dot(left, a_even[...])
        pb[...] += dot(left, b_even[...])
        return carry

    zero = jnp.zeros((8, 128), jnp.float32)
    sq, cross = lax.fori_loop(0, D // KB, block, (zero, zero))
    pa[...] += share * pb[...]

    pair = jnp.concatenate(
        [jnp.sum(sq, axis=0, keepdims=True), jnp.sum(cross, axis=0, keepdims=True)], axis=0)
    at = lax.broadcasted_iota(jnp.int32, (rows, 128), 0)
    lane = lax.broadcasted_iota(jnp.int32, (rows, 128), 1)

    def score_step(i, _):
        rs = pl.ds(pl.multiple_of(i * rows, rows), rows)
        out = []
        for ref in (pa, pb):
            part = fold_lanes(p_s[rs, :] * ref[rs, :])
            total = jnp.sum(part, axis=1, keepdims=True)
            out.append(jnp.sum(jnp.where(at == lane, total, 0.0), axis=0, keepdims=True))
        mine[i] = jnp.concatenate(out + [pair], axis=0)
        return 0

    def fold_lanes(v):
        out = v[:, 0:128]
        for j in range(1, width // 128):
            out = out + v[:, j * 128:(j + 1) * 128]
        return out

    lax.fori_loop(0, n, score_step, 0, unroll=4)

    def send(k):
        o = lax.rem(me + k, n)
        return pltpu.make_async_remote_copy(
            src_ref=mine.at[o], dst_ref=inbox.at[n - 1 - k],
            send_sem=ss, recv_sem=sr,
            device_id={"dp": o}, device_id_type=MESH)

    def all_sent():
        return pltpu.make_async_remote_copy(
            src_ref=mine.at[pl.ds(0, n - 1)], dst_ref=inbox,
            send_sem=ss, recv_sem=sr,
            device_id={"dp": sibling}, device_id_type=MESH)

    for k in range(1, n):
        send(k).start()

    def bent_step(i, _):
        rs = pl.ds(pl.multiple_of(i * STRIP, STRIP), STRIP)
        pa[rs, :] = q_s[rs, :] * pa[rs, :]
        pb[rs, :] = q_s[rs, :] * pb[rs, :]
        return 0

    lax.fori_loop(0, tokens // STRIP, bent_step, 0, unroll=4)

    def sent_line(i, _):
        o = (i * wide + y) * 2 + core

        def sent(up):
            pltpu.make_async_remote_copy(
                src_ref=slab(o), dst_ref=slab(o), send_sem=zs.at[0 if up else 1, o], recv_sem=zr.at[0, o],
                device_id={"dp": me + stride if up else me - stride}, device_id_type=MESH).wait_send()

        @pl.when((i <= z) & more)
        def _():
            sent(True)

        @pl.when((i >= z) & less)
        def _():
            sent(False)

        if wide == 2:
            over(o).wait_send()
        return 0

    lax.fori_loop(0, line, sent_line, 0)
    beside_all().wait_send()
    all_sent().wait_recv()

    tot = mine[me]
    for o in range(n - 1):
        tot = tot + inbox[o]
    sq = 0.2 * jnp.sum(tot[2:3], keepdims=True)
    cross = math.sqrt(0.2) * jnp.sum(tot[3:4], keepdims=True)
    rms = jnp.sqrt(sq / COUNT)
    scale = 1.0 / jnp.maximum(1.0, rms)
    bind = jnp.where(rms > 1.0, 1.0 / (rms * rms * rms), 0.0)
    alpha = (-0.01 * 0.1 * math.sqrt(20.0)) * scale
    beta = (0.01 * 0.2) * cross * bind / COUNT
    score_out[...] = alpha * tot[0:1] + beta * tot[1:2]
    alpha = jnp.broadcast_to(alpha, (STRIP, width))
    beta = jnp.broadcast_to(beta, (STRIP, width))

    def last_step(i, _):
        rs = pl.ds(pl.multiple_of(i * STRIP, STRIP), STRIP)
        bent_out[rs, :] = (alpha * pa[rs, :] + beta * pb[rs, :]).astype(jnp.bfloat16)
        return 0

    lax.fori_loop(0, tokens // STRIP, last_step, 0, unroll=4)
    all_sent().wait_send()


def last_kernel(tok, bent, adj, sc, theta_hbm, score, theta, out_sem):
    step = D // LAST
    parts = [pl.ds(i * step, step) for i in range(LAST)]
    outs = [pltpu.make_async_copy(theta.at[p, :], theta_hbm.at[p, :], out_sem.at[i]) for i, p in enumerate(parts)]
    for i, p in enumerate(parts):
        theta[p, :] = 0.999 * adj[p, :] + dot_rows(tok[:, p], bent[...])
        outs[i].start()
    score[...] = sc[:, :score.shape[1]]
    for copy in outs:
        copy.wait()


def shards(n, wide, x, cotangent, token_weight, weight, moment_one, moment_two, adjoint):
    rows = x.shape[0]
    tokens = n * rows
    width = weight.shape[1]
    pieces = 4 if n <= 16 else 1
    f32, bf16 = jnp.float32, jnp.bfloat16
    vm = pl.BlockSpec(memory_space=pltpu.VMEM)
    hbm = pl.BlockSpec(memory_space=pltpu.HBM)
    dma = pltpu.SemaphoreType.DMA
    tok, adj, bent, sc = pl.pallas_call(
        functools.partial(main_kernel, n, wide, pieces),
        out_shape=(
            pltpu.VMEM((tokens, D), bf16),
            pltpu.VMEM((D, width), f32),
            pltpu.VMEM((tokens, width), bf16),
            pltpu.VMEM((1, 128), f32),
        ),
        in_specs=[hbm] * 7,
        out_specs=(vm, vm, vm, vm),
        scratch_shapes=[
            pltpu.VMEM((tokens, width), bf16),
            pltpu.VMEM((1, tokens), f32),
            pltpu.VMEM((D, width), bf16),
            pltpu.VMEM((D, width), bf16),
            pltpu.VMEM((D, width), bf16),
            pltpu.VMEM((tokens, width), f32),
            pltpu.VMEM((tokens, width), f32),
            pltpu.VMEM((tokens, width), f32),
            pltpu.VMEM((tokens, width), bf16),
            pltpu.VMEM((KB, width), f32),
            pltpu.VMEM((KB, width), bf16),
            pltpu.VMEM((KB, width), bf16),
            pltpu.VMEM((tokens, width), f32),
            pltpu.VMEM((tokens, width), f32),
            pltpu.VMEM((n, 4, 128), f32),
            pltpu.VMEM((n - 1, 4, 128), f32),
            dma((3,)),
            dma((3, D // KB)),
            dma,
            dma((2, n)),
            dma((pieces, n)),
            dma((n,)),
            dma((n,)),
            dma,
            dma,
            dma,
            dma,
        ],
        compiler_params=pltpu.CompilerParams(
            collective_id=0, has_side_effects=True, vmem_limit_bytes=36 * 2**20
        ),
    )(*(
        pltpu.with_memory_space_constraint(a, pltpu.HBM)
        for a in (x, cotangent, token_weight.reshape(1, tokens), weight, moment_one, moment_two, adjoint)
    ))
    theta, score = pl.pallas_call(
        last_kernel,
        out_shape=(
            jax.ShapeDtypeStruct((D, width), f32),
            jax.ShapeDtypeStruct((1, rows), f32),
        ),
        in_specs=[vm] * 4,
        out_specs=(hbm, vm),
        scratch_shapes=[pltpu.VMEM((D, width), f32), dma((LAST,))],
        compiler_params=pltpu.CompilerParams(vmem_limit_bytes=36 * 2**20),
    )(tok, bent, adj, sc)
    return theta, score.reshape(rows)


def solution(mesh):
    n = mesh.shape["dp"]
    wide = 2 if mesh.shape["group"] == 2 else 1
    in_specs = (
        P(("group", "dp"), None),
        P("group", "dp"),
        P("group"),
        P(None, "dp"),
        P(None, "dp"),
        P(None, "dp"),
        P(None, "dp"),
    )
    out_specs = (P("group", "dp"), P(("group", "dp")))
    return jax.shard_map(
        functools.partial(shards, n, wide), mesh=mesh,
        in_specs=in_specs, out_specs=out_specs, check_vma=False)
```

```python
import functools
import math

import jax
import jax.numpy as jnp
from jax import lax
from jax.experimental import pallas as pl
from jax.experimental.pallas import tpu as pltpu
from jax.sharding import PartitionSpec as P

D = 4096
FW = 8192
COUNT = D * FW
MESH = pl.DeviceIdType.MESH
KB = 2048
STRIP = 16
LAST = 16
EPS = math.sqrt(20.0) * 1e-08


def dot(a, b):
    return jnp.dot(a, b, preferred_element_type=jnp.float32)


def dot_rows(a, b):
    return lax.dot_general(a, b, (((0,), (0,)), ((), ())), preferred_element_type=jnp.float32)


def main_kernel(
    n, wide, pieces,
    x_hbm, cot_hbm, tw_hbm, w_hbm, one_hbm, two_hbm, adj_hbm,
    tok, adj, bent_out, score_out,
    cot, tw_s, w, one, two, gate_s, p_s, q_s, scaled_s, g_even,
    a_even, b_even, pa, pb, mine, inbox,
    load_sem, block_sem, own_sem, zs, zr, ys, yr, cs, cr, ss, sr,
):
    me = lax.axis_index("dp")
    line = n // (2 * wide)
    core = lax.rem(me, 2)
    y = lax.rem(me // 2, wide)
    z = me // (2 * wide)
    stride = 2 * wide
    sibling = me + 1 - 2 * core
    across = me + (1 - 2 * y) * 2
    rows = x_hbm.shape[0]
    tokens, width = scaled_s.shape
    cols = D // pieces
    more, less = z + 1 < line, z > 0

    first_loads = [
        pltpu.make_async_copy(src, dst, load_sem.at[i])
        for i, (src, dst) in enumerate(((w_hbm, w), (cot_hbm, cot), (tw_hbm, tw_s)))
    ]

    def block_loads(i):
        p = pl.ds(pl.multiple_of(i * KB, KB), KB)
        return [
            pltpu.make_async_copy(src.at[p, :], dst.at[p, :], block_sem.at[j, i])
            for j, (src, dst) in enumerate(((two_hbm, two), (one_hbm, one), (adj_hbm, adj)))
        ]

    def slab(o):
        return tok.at[pl.ds(pl.multiple_of(o * rows, rows), rows), :]

    def piece(ref, h):
        return ref.at[:, pl.ds(h * cols, cols)]

    own = pltpu.make_async_copy(x_hbm, slab(me), own_sem)

    barrier = pltpu.get_barrier_semaphore()

    def greet(dev):
        pl.semaphore_signal(barrier, inc=1, device_id={"dp": dev}, device_id_type=MESH)

    greet(sibling)
    if wide == 2:
        greet(across)

    @pl.when(more)
    def _():
        greet(me + stride)

    @pl.when(less)
    def _():
        greet(me - stride)

    own.start()
    pl.semaphore_wait(barrier, wide + more.astype(jnp.int32) + less.astype(jnp.int32))

    def along(up, o, h, src=None):
        return pltpu.make_async_remote_copy(
            src_ref=piece(slab(o) if src is None else src, h), dst_ref=piece(slab(o), h),
            send_sem=zs.at[0 if up else 1, o], recv_sem=zr.at[h, o],
            device_id={"dp": me + stride if up else me - stride}, device_id_type=MESH)

    def over(o, h=None, src=None):
        src = slab(o) if src is None else src
        return pltpu.make_async_remote_copy(
            src_ref=src if h is None else piece(src, h), dst_ref=slab(o) if h is None else piece(slab(o), h),
            send_sem=ys.at[o], recv_sem=yr.at[o],
            device_id={"dp": across}, device_id_type=MESH)

    def beside(o, src=None):
        return pltpu.make_async_remote_copy(
            src_ref=slab(o) if src is None else src, dst_ref=slab(o),
            send_sem=cs, recv_sem=cr,
            device_id={"dp": sibling}, device_id_type=MESH)

    def beside_all():
        half = tok.at[pl.ds(0, tokens // 2), :]
        return pltpu.make_async_remote_copy(
            src_ref=half, dst_ref=half, send_sem=cs, recv_sem=cr,
            device_id={"dp": sibling}, device_id_type=MESH)

    for h in range(pieces):
        @pl.when(more)
        def _():
            along(True, me, h, x_hbm).start()

        @pl.when(less)
        def _():
            along(False, me, h, x_hbm).start()

        if wide == 2:
            over(me, h, x_hbm).start()
    beside(me, x_hbm).start()
    for copy in first_loads:
        copy.start()

    def from_across(k):
        if wide != 2:
            return
        for way in (-1, 1) if k else (1,):
            o = across + way * k * stride

            @pl.when((z + way * k >= 0) & (z + way * k < line))
            def _():
                over(o).wait_recv()
                beside(o).start()

    for k in range(1, line):
        for h in range(pieces):
            for way, onward in ((-1, more), (1, less)):
                o = me + way * k * stride

                @pl.when((z + way * k >= 0) & (z + way * k < line))
                def _():
                    along(way < 0, o, h).wait_recv()

                    @pl.when(onward)
                    def _():
                        along(way < 0, o, h).start()

                    if wide == 2:
                        over(o, h).start()
                    if h == pieces - 1:
                        beside(o).start()

        if k == line - 1:
            for i in range(D // KB):
                for copy in block_loads(i):
                    copy.start()
        from_across(k - 1)
    from_across(line - 1)
    beside_all().wait_recv()
    own.wait()
    for copy in first_loads:
        copy.wait()
    gate_s[...] = dot(tok[...], w[...])

    tw = jnp.transpose(jnp.broadcast_to(tw_s[...], (128, tokens)))
    q_s[:, 0:128] = tw

    def slope_step(i, _):
        rs = pl.ds(pl.multiple_of(i * STRIP, STRIP), STRIP)
        tw = q_s[rs, 0:128]
        for j in range(width // 128):
            js = slice(j * 128, (j + 1) * 128)
            gate = gate_s[rs, js]
            cot_f = cot[rs, js].astype(jnp.float32)
            sig = jax.nn.sigmoid(gate)
            slope = sig * (1.0 + gate * (1.0 - sig))
            curve = sig * (1.0 - sig) * (2.0 + gate * (1.0 - 2.0 * sig))
            scaled_s[rs, js] = (tw * cot_f * slope).astype(jnp.bfloat16)
            p_s[rs, js] = cot_f * slope
            q_s[rs, js] = tw * cot_f * curve
        return 0

    lax.fori_loop(0, tokens // STRIP, slope_step, 0, unroll=4)

    def fold(v):
        out = None
        for i in range(v.shape[0] // 8):
            for j in range(width // 128):
                part = v[i * 8:(i + 1) * 8, j * 128:(j + 1) * 128]
                out = part if out is None else out + part
        return out

    def fields(rs, g):
        second = 19.0 * two[rs, :].astype(jnp.float32) + g * g
        inv_root = lax.rsqrt(second)
        den = second * inv_root + EPS
        inv = lax.rsqrt(den * den)
        upd = (9.0 * one[rs, :].astype(jnp.float32) + g) * inv
        return inv_root, inv, upd

    def columns(i):
        return pl.ds(pl.multiple_of(i * KB, KB), KB)

    def strip(i, r):
        return pl.ds(pl.multiple_of(i * KB + r, STRIP), STRIP)

    def grad(i, out):
        out[...] = dot_rows(tok[:, columns(i)], scaled_s[...])

    grad(0, g_even)
    for copy in block_loads(0):
        copy.wait()
    sq = cross = jnp.zeros((8, 128), jnp.float32)
    for r in range(0, KB, KB // 4):
        _, _, upd = fields(strip(0, r), g_even[r:r + STRIP, :])
        sq = sq + fold(upd * upd)
        cross = cross + fold(adj[strip(0, r), :] * upd)
    share = jnp.sum(cross, keepdims=True) / (jnp.sum(sq, keepdims=True) + 1e-03)

    pa[...] = jnp.zeros_like(pa)
    pb[...] = jnp.zeros_like(pb)

    def block(i, carry):
        base = i * KB

        @pl.when(i > 0)
        def _():
            grad(i, g_even)
            for copy in block_loads(i):
                copy.wait()

        def fill(r, carry):
            sq, cross = carry
            here = pl.ds(pl.multiple_of(r * 16, 16), 16)
            rs = pl.ds(pl.multiple_of(base + r * 16, 16), 16)
            g = g_even[here, :]
            inv_root, inv, upd = fields(rs, g)
            slope = inv - inv * ((g * inv_root) * upd)
            adj_r = adj[rs, :]
            sq = sq + fold(upd * upd)
            cross = cross + fold(adj_r * upd)
            a_even[here, :] = ((adj_r - share * upd) * slope).astype(jnp.bfloat16)
            b_even[here, :] = (upd * slope).astype(jnp.bfloat16)
            return sq, cross

        carry = lax.fori_loop(0, KB // 16, fill, carry, unroll=4)
        left = tok[:, columns(i)]
        pa[...] += dot(left, a_even[...])
        pb[...] += dot(left, b_even[...])
        return carry

    zero = jnp.zeros((8, 128), jnp.float32)
    sq, cross = lax.fori_loop(0, D // KB, block, (zero, zero))
    pa[...] += share * pb[...]

    pair = jnp.concatenate(
        [jnp.sum(sq, axis=0, keepdims=True), jnp.sum(cross, axis=0, keepdims=True)], axis=0)
    at = lax.broadcasted_iota(jnp.int32, (rows, 128), 0)
    lane = lax.broadcasted_iota(jnp.int32, (rows, 128), 1)

    def score_step(i, _):
        rs = pl.ds(pl.multiple_of(i * rows, rows), rows)
        out = []
        for ref in (pa, pb):
            part = fold_lanes(p_s[rs, :] * ref[rs, :])
            total = jnp.sum(part, axis=1, keepdims=True)
            out.append(jnp.sum(jnp.where(at == lane, total, 0.0), axis=0, keepdims=True))
        mine[i] = jnp.concatenate(out + [pair], axis=0)
        return 0

    def fold_lanes(v):
        out = v[:, 0:128]
        for j in range(1, width // 128):
            out = out + v[:, j * 128:(j + 1) * 128]
        return out

    lax.fori_loop(0, n, score_step, 0, unroll=4)

    def send(k):
        o = lax.rem(me + k, n)
        return pltpu.make_async_remote_copy(
            src_ref=mine.at[o], dst_ref=inbox.at[n - 1 - k],
            send_sem=ss, recv_sem=sr,
            device_id={"dp": o}, device_id_type=MESH)

    def all_sent():
        return pltpu.make_async_remote_copy(
            src_ref=mine.at[pl.ds(0, n - 1)], dst_ref=inbox,
            send_sem=ss, recv_sem=sr,
            device_id={"dp": sibling}, device_id_type=MESH)

    for k in range(1, n):
        send(k).start()

    def bent_step(i, _):
        rs = pl.ds(pl.multiple_of(i * STRIP, STRIP), STRIP)
        pa[rs, :] = q_s[rs, :] * pa[rs, :]
        pb[rs, :] = q_s[rs, :] * pb[rs, :]
        return 0

    lax.fori_loop(0, tokens // STRIP, bent_step, 0, unroll=4)

    def sent_line(i, _):
        o = (i * wide + y) * 2 + core

        def sent(up):
            pltpu.make_async_remote_copy(
                src_ref=slab(o), dst_ref=slab(o), send_sem=zs.at[0 if up else 1, o], recv_sem=zr.at[0, o],
                device_id={"dp": me + stride if up else me - stride}, device_id_type=MESH).wait_send()

        @pl.when((i <= z) & more)
        def _():
            sent(True)

        @pl.when((i >= z) & less)
        def _():
            sent(False)

        if wide == 2:
            over(o).wait_send()
        return 0

    lax.fori_loop(0, line, sent_line, 0)
    beside_all().wait_send()
    all_sent().wait_recv()

    tot = mine[me]
    for o in range(n - 1):
        tot = tot + inbox[o]
    sq = 0.2 * jnp.sum(tot[2:3], keepdims=True)
    cross = math.sqrt(0.2) * jnp.sum(tot[3:4], keepdims=True)
    rms = jnp.sqrt(sq / COUNT)
    scale = 1.0 / jnp.maximum(1.0, rms)
    bind = jnp.where(rms > 1.0, 1.0 / (rms * rms * rms), 0.0)
    alpha = (-0.01 * 0.1 * math.sqrt(20.0)) * scale
    beta = (0.01 * 0.2) * cross * bind / COUNT
    score_out[...] = alpha * tot[0:1] + beta * tot[1:2]
    alpha = jnp.broadcast_to(alpha, (STRIP, width))
    beta = jnp.broadcast_to(beta, (STRIP, width))

    def last_step(i, _):
        rs = pl.ds(pl.multiple_of(i * STRIP, STRIP), STRIP)
        bent_out[rs, :] = (alpha * pa[rs, :] + beta * pb[rs, :]).astype(jnp.bfloat16)
        return 0

    lax.fori_loop(0, tokens // STRIP, last_step, 0, unroll=4)
    all_sent().wait_send()


def last_kernel(tok, bent, adj, sc, theta_hbm, score, theta, out_sem):
    step = D // LAST
    parts = [pl.ds(i * step, step) for i in range(LAST)]
    outs = [pltpu.make_async_copy(theta.at[p, :], theta_hbm.at[p, :], out_sem.at[i]) for i, p in enumerate(parts)]
    for i, p in enumerate(parts):
        theta[p, :] = 0.999 * adj[p, :] + dot_rows(tok[:, p], bent[...])
        outs[i].start()
    score[...] = sc[:, :score.shape[1]]
    for copy in outs:
        copy.wait()


def shards(n, wide, x, cotangent, token_weight, weight, moment_one, moment_two, adjoint):
    rows = x.shape[0]
    tokens = n * rows
    width = weight.shape[1]
    pieces = 4 if n <= 16 else 1
    f32, bf16 = jnp.float32, jnp.bfloat16
    vm = pl.BlockSpec(memory_space=pltpu.VMEM)
    hbm = pl.BlockSpec(memory_space=pltpu.HBM)
    dma = pltpu.SemaphoreType.DMA
    tok, adj, bent, sc = pl.pallas_call(
        functools.partial(main_kernel, n, wide, pieces),
        out_shape=(
            pltpu.VMEM((tokens, D), bf16),
            pltpu.VMEM((D, width), f32),
            pltpu.VMEM((tokens, width), bf16),
            pltpu.VMEM((1, 128), f32),
        ),
        in_specs=[hbm] * 7,
        out_specs=(vm, vm, vm, vm),
        scratch_shapes=[
            pltpu.VMEM((tokens, width), bf16),
            pltpu.VMEM((1, tokens), f32),
            pltpu.VMEM((D, width), bf16),
            pltpu.VMEM((D, width), bf16),
            pltpu.VMEM((D, width), bf16),
            pltpu.VMEM((tokens, width), f32),
            pltpu.VMEM((tokens, width), f32),
            pltpu.VMEM((tokens, width), f32),
            pltpu.VMEM((tokens, width), bf16),
            pltpu.VMEM((KB, width), f32),
            pltpu.VMEM((KB, width), bf16),
            pltpu.VMEM((KB, width), bf16),
            pltpu.VMEM((tokens, width), f32),
            pltpu.VMEM((tokens, width), f32),
            pltpu.VMEM((n, 4, 128), f32),
            pltpu.VMEM((n - 1, 4, 128), f32),
            dma((3,)),
            dma((3, D // KB)),
            dma,
            dma((2, n)),
            dma((pieces, n)),
            dma((n,)),
            dma((n,)),
            dma,
            dma,
            dma,
            dma,
        ],
        compiler_params=pltpu.CompilerParams(
            collective_id=0, has_side_effects=True, vmem_limit_bytes=36 * 2**20
        ),
    )(*(
        pltpu.with_memory_space_constraint(a, pltpu.HBM)
        for a in (x, cotangent, token_weight.reshape(1, tokens), weight, moment_one, moment_two, adjoint)
    ))
    theta, score = pl.pallas_call(
        last_kernel,
        out_shape=(
            jax.ShapeDtypeStruct((D, width), f32),
            jax.ShapeDtypeStruct((1, rows), f32),
        ),
        in_specs=[vm] * 4,
        out_specs=(hbm, vm),
        scratch_shapes=[pltpu.VMEM((D, width), f32), dma((LAST,))],
        compiler_params=pltpu.CompilerParams(vmem_limit_bytes=36 * 2**20),
    )(tok, bent, adj, sc)
    return theta, score.reshape(rows)


def solution(mesh):
    n = mesh.shape["dp"]
    wide = 2 if mesh.shape["group"] == 2 else 1
    in_specs = (
        P(("group", "dp"), None),
        P("group", "dp"),
        P("group"),
        P(None, "dp"),
        P(None, "dp"),
        P(None, "dp"),
        P(None, "dp"),
    )
    out_specs = (P("group", "dp"), P(("group", "dp")))
    return jax.shard_map(
        functools.partial(shards, n, wide), mesh=mesh,
        in_specs=in_specs, out_specs=out_specs, check_vma=False)
```

```python
import functools
import math

import jax
import jax.numpy as jnp
from jax import lax
from jax.experimental import pallas as pl
from jax.experimental.pallas import tpu as pltpu
from jax.sharding import PartitionSpec as P

D = 4096
FW = 8192
COUNT = D * FW
MESH = pl.DeviceIdType.MESH
KB = 2048
STRIP = 16
LAST = 16
EPS = math.sqrt(20.0) * 1e-08


def dot(a, b):
    return jnp.dot(a, b, preferred_element_type=jnp.float32)


def dot_rows(a, b):
    return lax.dot_general(a, b, (((0,), (0,)), ((), ())), preferred_element_type=jnp.float32)


def main_kernel(
    n, wide, pieces,
    x_hbm, cot_hbm, tw_hbm, w_hbm, one_hbm, two_hbm, adj_hbm,
    tok, adj, bent_out, score_out,
    cot, tw_s, w, one, two, gate_s, p_s, q_s, scaled_s, g_even,
    a_even, b_even, pa, pb, mine, inbox,
    load_sem, block_sem, own_sem, zs, zr, ys, yr, cs, cr, ss, sr,
):
    me = lax.axis_index("dp")
    line = n // (2 * wide)
    core = lax.rem(me, 2)
    y = lax.rem(me // 2, wide)
    z = me // (2 * wide)
    stride = 2 * wide
    sibling = me + 1 - 2 * core
    across = me + (1 - 2 * y) * 2
    rows = x_hbm.shape[0]
    tokens, width = scaled_s.shape
    cols = D // pieces
    more, less = z + 1 < line, z > 0

    first_loads = [
        pltpu.make_async_copy(src, dst, load_sem.at[i])
        for i, (src, dst) in enumerate(((w_hbm, w), (cot_hbm, cot), (tw_hbm, tw_s)))
    ]

    def block_loads(i):
        p = pl.ds(pl.multiple_of(i * KB, KB), KB)
        return [
            pltpu.make_async_copy(src.at[p, :], dst.at[p, :], block_sem.at[j, i])
            for j, (src, dst) in enumerate(((two_hbm, two), (one_hbm, one), (adj_hbm, adj)))
        ]

    def slab(o):
        return tok.at[pl.ds(pl.multiple_of(o * rows, rows), rows), :]

    def piece(ref, h):
        return ref.at[:, pl.ds(h * cols, cols)]

    own = pltpu.make_async_copy(x_hbm, slab(me), own_sem)

    barrier = pltpu.get_barrier_semaphore()

    def greet(dev):
        pl.semaphore_signal(barrier, inc=1, device_id={"dp": dev}, device_id_type=MESH)

    greet(sibling)
    if wide == 2:
        greet(across)

    @pl.when(more)
    def _():
        greet(me + stride)

    @pl.when(less)
    def _():
        greet(me - stride)

    own.start()
    pl.semaphore_wait(barrier, wide + more.astype(jnp.int32) + less.astype(jnp.int32))

    def along(up, o, h, src=None):
        return pltpu.make_async_remote_copy(
            src_ref=piece(slab(o) if src is None else src, h), dst_ref=piece(slab(o), h),
            send_sem=zs.at[0 if up else 1, o], recv_sem=zr.at[h, o],
            device_id={"dp": me + stride if up else me - stride}, device_id_type=MESH)

    def over(o, h=None, src=None):
        src = slab(o) if src is None else src
        return pltpu.make_async_remote_copy(
            src_ref=src if h is None else piece(src, h), dst_ref=slab(o) if h is None else piece(slab(o), h),
            send_sem=ys.at[o], recv_sem=yr.at[o],
            device_id={"dp": across}, device_id_type=MESH)

    def beside(o, src=None):
        return pltpu.make_async_remote_copy(
            src_ref=slab(o) if src is None else src, dst_ref=slab(o),
            send_sem=cs, recv_sem=cr,
            device_id={"dp": sibling}, device_id_type=MESH)

    def beside_all():
        half = tok.at[pl.ds(0, tokens // 2), :]
        return pltpu.make_async_remote_copy(
            src_ref=half, dst_ref=half, send_sem=cs, recv_sem=cr,
            device_id={"dp": sibling}, device_id_type=MESH)

    for h in range(pieces):
        @pl.when(more)
        def _():
            along(True, me, h, x_hbm).start()

        @pl.when(less)
        def _():
            along(False, me, h, x_hbm).start()

        if wide == 2:
            over(me, h, x_hbm).start()
    beside(me, x_hbm).start()
    for copy in first_loads:
        copy.start()

    def from_across(k):
        if wide != 2:
            return
        for way in (-1, 1) if k else (1,):
            o = across + way * k * stride

            @pl.when((z + way * k >= 0) & (z + way * k < line))
            def _():
                over(o).wait_recv()
                beside(o).start()

    for k in range(1, line):
        for h in range(pieces):
            for way, onward in ((-1, more), (1, less)):
                o = me + way * k * stride

                @pl.when((z + way * k >= 0) & (z + way * k < line))
                def _():
                    along(way < 0, o, h).wait_recv()

                    @pl.when(onward)
                    def _():
                        along(way < 0, o, h).start()

                    if wide == 2:
                        over(o, h).start()
                    if h == pieces - 1:
                        beside(o).start()

        if k == line - 1:
            for i in range(D // KB):
                for copy in block_loads(i):
                    copy.start()
        from_across(k - 1)
    from_across(line - 1)
    beside_all().wait_recv()
    own.wait()
    for copy in first_loads:
        copy.wait()
    gate_s[...] = dot(tok[...], w[...])

    tw = jnp.transpose(jnp.broadcast_to(tw_s[...], (128, tokens)))
    q_s[:, 0:128] = tw

    def slope_step(i, _):
        rs = pl.ds(pl.multiple_of(i * STRIP, STRIP), STRIP)
        tw = q_s[rs, 0:128]
        for j in range(width // 128):
            js = slice(j * 128, (j + 1) * 128)
            gate = gate_s[rs, js]
            cot_f = cot[rs, js].astype(jnp.float32)
            sig = jax.nn.sigmoid(gate)
            slope = sig * (1.0 + gate * (1.0 - sig))
            curve = sig * (1.0 - sig) * (2.0 + gate * (1.0 - 2.0 * sig))
            scaled_s[rs, js] = (tw * cot_f * slope).astype(jnp.bfloat16)
            p_s[rs, js] = cot_f * slope
            q_s[rs, js] = tw * cot_f * curve
        return 0

    lax.fori_loop(0, tokens // STRIP, slope_step, 0, unroll=4)

    def fold(v):
        out = None
        for i in range(v.shape[0] // 8):
            for j in range(width // 128):
                part = v[i * 8:(i + 1) * 8, j * 128:(j + 1) * 128]
                out = part if out is None else out + part
        return out

    def fields(rs, g):
        second = 19.0 * two[rs, :].astype(jnp.float32) + g * g
        inv_root = lax.rsqrt(second)
        den = second * inv_root + EPS
        inv = lax.rsqrt(den * den)
        upd = (9.0 * one[rs, :].astype(jnp.float32) + g) * inv
        return inv_root, inv, upd

    def columns(i):
        return pl.ds(pl.multiple_of(i * KB, KB), KB)

    def strip(i, r):
        return pl.ds(pl.multiple_of(i * KB + r, STRIP), STRIP)

    def grad(i, out):
        out[...] = dot_rows(tok[:, columns(i)], scaled_s[...])

    grad(0, g_even)
    for copy in block_loads(0):
        copy.wait()
    sq = cross = jnp.zeros((8, 128), jnp.float32)
    for r in range(0, KB, KB // 4):
        _, _, upd = fields(strip(0, r), g_even[r:r + STRIP, :])
        sq = sq + fold(upd * upd)
        cross = cross + fold(adj[strip(0, r), :] * upd)
    share = jnp.sum(cross, keepdims=True) / (jnp.sum(sq, keepdims=True) + 1e-03)


    def block(i, carry):
        base = i * KB
        if i > 0:
            grad(i, g_even)
            for copy in block_loads(i):
                copy.wait()

        def fill(r, carry):
            sq, cross = carry
            here = pl.ds(pl.multiple_of(r * 16, 16), 16)
            rs = pl.ds(pl.multiple_of(base + r * 16, 16), 16)
            g = g_even[here, :]
            inv_root, inv, upd = fields(rs, g)
            slope = inv - inv * ((g * inv_root) * upd)
            adj_r = adj[rs, :]
            sq = sq + fold(upd * upd)
            cross = cross + fold(adj_r * upd)
            a_even[here, :] = ((adj_r - share * upd) * slope).astype(jnp.bfloat16)
            b_even[here, :] = (upd * slope).astype(jnp.bfloat16)
            return sq, cross

        carry = lax.fori_loop(0, KB // 16, fill, carry, unroll=4)
        left = tok[:, columns(i)]
        if i == 0:
            pa[...] = dot(left, a_even[...])
            pb[...] = dot(left, b_even[...])
        else:
            pa[...] += dot(left, a_even[...])
            pb[...] += dot(left, b_even[...])
        return carry

    zero = jnp.zeros((8, 128), jnp.float32)
    carry = (zero, zero)
    for i in range(D // KB):
        carry = block(i, carry)
    sq, cross = carry
    pa[...] += share * pb[...]

    spans = tokens // 128

    def token_sums(ref):
        out = []
        for i in range(tokens // 128):
            rs = slice(i * 128, (i + 1) * 128)
            part = p_s[rs, 0:128] * ref[rs, 0:128]
            for j in range(1, width // 128):
                js = slice(j * 128, (j + 1) * 128)
                part = part + p_s[rs, js] * ref[rs, js]
            out.append(jnp.sum(jnp.transpose(part), axis=0, keepdims=True))
        return out

    mine[...] = jnp.concatenate(
        token_sums(pa) + token_sums(pb)
        + [jnp.sum(sq, axis=0, keepdims=True), jnp.sum(cross, axis=0, keepdims=True)], axis=0)

    def send(k):
        o = lax.rem(me + k, n)
        return pltpu.make_async_remote_copy(
            src_ref=mine, dst_ref=inbox.at[n - 1 - k],
            send_sem=ss, recv_sem=sr,
            device_id={"dp": o}, device_id_type=MESH)

    def all_sent():
        return pltpu.make_async_remote_copy(
            src_ref=inbox, dst_ref=inbox,
            send_sem=ss, recv_sem=sr,
            device_id={"dp": sibling}, device_id_type=MESH)

    for k in range(1, n):
        send(k).start()

    def bent_step(i, _):
        rs = pl.ds(pl.multiple_of(i * STRIP, STRIP), STRIP)
        pa[rs, :] = q_s[rs, :] * pa[rs, :]
        pb[rs, :] = q_s[rs, :] * pb[rs, :]
        return 0

    lax.fori_loop(0, tokens // STRIP, bent_step, 0, unroll=4)

    def sent_line(i, _):
        o = (i * wide + y) * 2 + core

        def sent(up):
            pltpu.make_async_remote_copy(
                src_ref=slab(o), dst_ref=slab(o), send_sem=zs.at[0 if up else 1, o], recv_sem=zr.at[0, o],
                device_id={"dp": me + stride if up else me - stride}, device_id_type=MESH).wait_send()

        @pl.when((i <= z) & more)
        def _():
            sent(True)

        @pl.when((i >= z) & less)
        def _():
            sent(False)

        if wide == 2:
            over(o).wait_send()
        return 0

    lax.fori_loop(0, line, sent_line, 0)
    beside_all().wait_send()
    all_sent().wait_recv()

    tot = mine[...]
    for o in range(n - 1):
        tot = tot + inbox[o]
    sq = 0.2 * jnp.sum(tot[2 * spans:2 * spans + 1], keepdims=True)
    cross = math.sqrt(0.2) * jnp.sum(tot[2 * spans + 1:], keepdims=True)
    rms = jnp.sqrt(sq / COUNT)
    scale = 1.0 / jnp.maximum(1.0, rms)
    bind = jnp.where(rms > 1.0, 1.0 / (rms * rms * rms), 0.0)
    alpha = (-0.01 * 0.1 * math.sqrt(20.0)) * scale
    beta = (0.01 * 0.2) * cross * bind / COUNT
    scores = alpha * tot[0:spans] + beta * tot[spans:2 * spans]
    span = lax.broadcasted_iota(jnp.int32, (spans, 128), 0)
    scores = jnp.sum(jnp.where(span == me * rows // 128, scores, 0.0), axis=0, keepdims=True)
    lane = lax.broadcasted_iota(jnp.int32, (128, 128), 0) - lax.rem(me * rows, 128)
    at = lax.broadcasted_iota(jnp.int32, (128, 128), 1)
    column = jnp.transpose(jnp.broadcast_to(scores, (128, 128)))
    score_out[...] = jnp.sum(jnp.where(lane == at, column, 0.0), axis=0, keepdims=True)
    alpha = jnp.broadcast_to(alpha, (STRIP, width))
    beta = jnp.broadcast_to(beta, (STRIP, width))

    def last_step(i, _):
        rs = pl.ds(pl.multiple_of(i * STRIP, STRIP), STRIP)
        bent_out[rs, :] = (alpha * pa[rs, :] + beta * pb[rs, :]).astype(jnp.bfloat16)
        return 0

    lax.fori_loop(0, tokens // STRIP, last_step, 0, unroll=4)
    all_sent().wait_send()


def last_kernel(tok, bent, adj, sc, theta_hbm, score, theta, out_sem):
    step = D // LAST
    parts = [pl.ds(i * step, step) for i in range(LAST)]
    outs = [pltpu.make_async_copy(theta.at[p, :], theta_hbm.at[p, :], out_sem.at[i]) for i, p in enumerate(parts)]
    for i, p in enumerate(parts):
        theta[p, :] = 0.999 * adj[p, :] + dot_rows(tok[:, p], bent[...])
        outs[i].start()
    score[...] = sc[:, :score.shape[1]]
    for copy in outs:
        copy.wait()


def shards(n, wide, x, cotangent, token_weight, weight, moment_one, moment_two, adjoint):
    rows = x.shape[0]
    tokens = n * rows
    width = weight.shape[1]
    pieces = 4 if n <= 16 else 1
    f32, bf16 = jnp.float32, jnp.bfloat16
    vm = pl.BlockSpec(memory_space=pltpu.VMEM)
    hbm = pl.BlockSpec(memory_space=pltpu.HBM)
    dma = pltpu.SemaphoreType.DMA
    tok, adj, bent, sc = pl.pallas_call(
        functools.partial(main_kernel, n, wide, pieces),
        out_shape=(
            pltpu.VMEM((tokens, D), bf16),
            pltpu.VMEM((D, width), f32),
            pltpu.VMEM((tokens, width), bf16),
            pltpu.VMEM((1, 128), f32),
        ),
        in_specs=[hbm] * 7,
        out_specs=(vm, vm, vm, vm),
        scratch_shapes=[
            pltpu.VMEM((tokens, width), bf16),
            pltpu.VMEM((1, tokens), f32),
            pltpu.VMEM((D, width), bf16),
            pltpu.VMEM((D, width), bf16),
            pltpu.VMEM((D, width), bf16),
            pltpu.VMEM((tokens, width), f32),
            pltpu.VMEM((tokens, width), f32),
            pltpu.VMEM((tokens, width), f32),
            pltpu.VMEM((tokens, width), bf16),
            pltpu.VMEM((KB, width), f32),
            pltpu.VMEM((KB, width), bf16),
            pltpu.VMEM((KB, width), bf16),
            pltpu.VMEM((tokens, width), f32),
            pltpu.VMEM((tokens, width), f32),
            pltpu.VMEM((tokens // 64 + 2, 128), f32),
            pltpu.VMEM((n - 1, tokens // 64 + 2, 128), f32),
            dma((3,)),
            dma((3, D // KB)),
            dma,
            dma((2, n)),
            dma((pieces, n)),
            dma((n,)),
            dma((n,)),
            dma,
            dma,
            dma,
            dma,
        ],
        compiler_params=pltpu.CompilerParams(
            collective_id=0, has_side_effects=True, vmem_limit_bytes=36 * 2**20
        ),
    )(*(
        pltpu.with_memory_space_constraint(a, pltpu.HBM)
        for a in (x, cotangent, token_weight.reshape(1, tokens), weight, moment_one, moment_two, adjoint)
    ))
    theta, score = pl.pallas_call(
        last_kernel,
        out_shape=(
            jax.ShapeDtypeStruct((D, width), f32),
            jax.ShapeDtypeStruct((1, rows), f32),
        ),
        in_specs=[vm] * 4,
        out_specs=(hbm, vm),
        scratch_shapes=[pltpu.VMEM((D, width), f32), dma((LAST,))],
        compiler_params=pltpu.CompilerParams(vmem_limit_bytes=36 * 2**20),
    )(tok, bent, adj, sc)
    return theta, score.reshape(rows)


def solution(mesh):
    n = mesh.shape["dp"]
    wide = 2 if mesh.shape["group"] == 2 else 1
    in_specs = (
        P(("group", "dp"), None),
        P("group", "dp"),
        P("group"),
        P(None, "dp"),
        P(None, "dp"),
        P(None, "dp"),
        P(None, "dp"),
    )
    out_specs = (P("group", "dp"), P(("group", "dp")))
    return jax.shard_map(
        functools.partial(shards, n, wide), mesh=mesh,
        in_specs=in_specs, out_specs=out_specs, check_vma=False)
```

```python
import functools
import math

import jax
import jax.numpy as jnp
from jax import lax
from jax.experimental import pallas as pl
from jax.experimental.pallas import tpu as pltpu
from jax.sharding import PartitionSpec as P

D = 4096
FW = 8192
COUNT = D * FW
MESH = pl.DeviceIdType.MESH
KB = 2048
STRIP = 16
LAST = 16
EPS = math.sqrt(20.0) * 1e-08


def dot(a, b):
    return jnp.dot(a, b, preferred_element_type=jnp.float32)


def dot_rows(a, b):
    return lax.dot_general(a, b, (((0,), (0,)), ((), ())), preferred_element_type=jnp.float32)


def main_kernel(
    n, wide, pieces,
    x_hbm, cot_hbm, tw_hbm, w_hbm, one_hbm, two_hbm, adj_hbm,
    tok, adj, bent_out, score_out,
    cot, tw_s, w, one, two, gate_s, p_s, q_s, scaled_s, g_even,
    a_even, b_even, pa, pb, mine, inbox,
    load_sem, block_sem, own_sem, zs, zr, ys, yr, cs, cr, ss, sr,
):
    me = lax.axis_index("dp")
    line = n // (2 * wide)
    core = lax.rem(me, 2)
    y = lax.rem(me // 2, wide)
    z = me // (2 * wide)
    stride = 2 * wide
    sibling = me + 1 - 2 * core
    across = me + (1 - 2 * y) * 2
    rows = x_hbm.shape[0]
    tokens, width = scaled_s.shape
    cols = D // pieces
    more, less = z + 1 < line, z > 0

    first_loads = [
        pltpu.make_async_copy(src, dst, load_sem.at[i])
        for i, (src, dst) in enumerate(((w_hbm, w), (cot_hbm, cot), (tw_hbm, tw_s)))
    ]

    def block_loads(i):
        p = pl.ds(pl.multiple_of(i * KB, KB), KB)
        return [
            pltpu.make_async_copy(src.at[p, :], dst.at[p, :], block_sem.at[j, i])
            for j, (src, dst) in enumerate(((two_hbm, two), (one_hbm, one), (adj_hbm, adj)))
        ]

    def slab(o):
        return tok.at[pl.ds(pl.multiple_of(o * rows, rows), rows), :]

    def piece(ref, h):
        return ref.at[:, pl.ds(h * cols, cols)]

    own = pltpu.make_async_copy(x_hbm, slab(me), own_sem)

    barrier = pltpu.get_barrier_semaphore()

    def greet(dev):
        pl.semaphore_signal(barrier, inc=1, device_id={"dp": dev}, device_id_type=MESH)

    greet(sibling)
    if wide == 2:
        greet(across)

    @pl.when(more)
    def _():
        greet(me + stride)

    @pl.when(less)
    def _():
        greet(me - stride)

    own.start()
    pl.semaphore_wait(barrier, wide + more.astype(jnp.int32) + less.astype(jnp.int32))

    def along(up, o, h, src=None):
        return pltpu.make_async_remote_copy(
            src_ref=piece(slab(o) if src is None else src, h), dst_ref=piece(slab(o), h),
            send_sem=zs.at[0 if up else 1, o], recv_sem=zr.at[h, o],
            device_id={"dp": me + stride if up else me - stride}, device_id_type=MESH)

    def over(o, h=None, src=None):
        src = slab(o) if src is None else src
        return pltpu.make_async_remote_copy(
            src_ref=src if h is None else piece(src, h), dst_ref=slab(o) if h is None else piece(slab(o), h),
            send_sem=ys.at[o], recv_sem=yr.at[o],
            device_id={"dp": across}, device_id_type=MESH)

    def beside(o, src=None):
        return pltpu.make_async_remote_copy(
            src_ref=slab(o) if src is None else src, dst_ref=slab(o),
            send_sem=cs, recv_sem=cr,
            device_id={"dp": sibling}, device_id_type=MESH)

    def beside_all():
        half = tok.at[pl.ds(0, tokens // 2), :]
        return pltpu.make_async_remote_copy(
            src_ref=half, dst_ref=half, send_sem=cs, recv_sem=cr,
            device_id={"dp": sibling}, device_id_type=MESH)

    for h in range(pieces):
        @pl.when(more)
        def _():
            along(True, me, h, x_hbm).start()

        @pl.when(less)
        def _():
            along(False, me, h, x_hbm).start()

        if wide == 2:
            over(me, h, x_hbm).start()
    beside(me, x_hbm).start()
    for copy in first_loads:
        copy.start()

    def from_across(k):
        if wide != 2:
            return
        for way in (-1, 1) if k else (1,):
            o = across + way * k * stride

            @pl.when((z + way * k >= 0) & (z + way * k < line))
            def _():
                over(o).wait_recv()
                beside(o).start()

    for k in range(1, line):
        for h in range(pieces):
            for way, onward in ((-1, more), (1, less)):
                o = me + way * k * stride

                @pl.when((z + way * k >= 0) & (z + way * k < line))
                def _():
                    along(way < 0, o, h).wait_recv()

                    @pl.when(onward)
                    def _():
                        along(way < 0, o, h).start()

                    if wide == 2:
                        over(o, h).start()
                    if h == pieces - 1:
                        beside(o).start()

        if k == line - 1:
            for i in range(D // KB):
                for copy in block_loads(i):
                    copy.start()
        from_across(k - 1)
    from_across(line - 1)
    beside_all().wait_recv()
    own.wait()
    for copy in first_loads:
        copy.wait()
    gate_s[...] = dot(tok[...], w[...])

    tw = jnp.transpose(jnp.broadcast_to(tw_s[...], (128, tokens)))
    q_s[:, 0:128] = tw

    def slope_step(i, _):
        rs = pl.ds(pl.multiple_of(i * STRIP, STRIP), STRIP)
        tw = q_s[rs, 0:128]
        for j in range(width // 128):
            js = slice(j * 128, (j + 1) * 128)
            gate = gate_s[rs, js]
            cot_f = cot[rs, js].astype(jnp.float32)
            sig = jax.nn.sigmoid(gate)
            slope = sig * (1.0 + gate * (1.0 - sig))
            curve = sig * (1.0 - sig) * (2.0 + gate * (1.0 - 2.0 * sig))
            scaled_s[rs, js] = (tw * cot_f * slope).astype(jnp.bfloat16)
            p_s[rs, js] = cot_f * slope
            q_s[rs, js] = tw * cot_f * curve
        return 0

    lax.fori_loop(0, tokens // STRIP, slope_step, 0, unroll=4)

    def fold(v):
        out = None
        for i in range(v.shape[0] // 8):
            for j in range(width // 128):
                part = v[i * 8:(i + 1) * 8, j * 128:(j + 1) * 128]
                out = part if out is None else out + part
        return out

    def fields(rs, g):
        second = 19.0 * two[rs, :].astype(jnp.float32) + g * g
        inv_root = lax.rsqrt(second)
        den = second * inv_root + EPS
        inv = lax.rsqrt(den * den)
        upd = (9.0 * one[rs, :].astype(jnp.float32) + g) * inv
        return inv_root, inv, upd

    def columns(i):
        return pl.ds(pl.multiple_of(i * KB, KB), KB)

    def strip(i, r):
        return pl.ds(pl.multiple_of(i * KB + r, STRIP), STRIP)

    def grad(i, out):
        out[...] = dot_rows(tok[:, columns(i)], scaled_s[...])

    grad(0, g_even)
    for copy in block_loads(0):
        copy.wait()
    sq = cross = jnp.zeros((8, 128), jnp.float32)
    for r in range(0, KB, KB // 4):
        _, _, upd = fields(strip(0, r), g_even[r:r + STRIP, :])
        sq = sq + fold(upd * upd)
        cross = cross + fold(adj[strip(0, r), :] * upd)
    share = jnp.sum(cross, keepdims=True) / (jnp.sum(sq, keepdims=True) + 1e-03)


    def block(i, carry):
        base = i * KB
        if i > 0:
            grad(i, g_even)
            for copy in block_loads(i):
                copy.wait()

        def fill(r, carry):
            sq, cross = carry
            here = pl.ds(pl.multiple_of(r * 16, 16), 16)
            rs = pl.ds(pl.multiple_of(base + r * 16, 16), 16)
            g = g_even[here, :]
            inv_root, inv, upd = fields(rs, g)
            slope = inv - inv * ((g * inv_root) * upd)
            adj_r = adj[rs, :]
            sq = sq + fold(upd * upd)
            cross = cross + fold(adj_r * upd)
            a_even[here, :] = ((adj_r - share * upd) * slope).astype(jnp.bfloat16)
            b_even[here, :] = (upd * slope).astype(jnp.bfloat16)
            return sq, cross

        carry = lax.fori_loop(0, KB // 16, fill, carry, unroll=8)
        left = tok[:, columns(i)]
        if i == 0:
            pa[...] = dot(left, a_even[...])
            pb[...] = dot(left, b_even[...])
        else:
            pa[...] += dot(left, a_even[...])
            pb[...] += dot(left, b_even[...])
        return carry

    zero = jnp.zeros((8, 128), jnp.float32)
    carry = (zero, zero)
    for i in range(D // KB):
        carry = block(i, carry)
    sq, cross = carry
    pa[...] += share * pb[...]

    spans = tokens // 128

    def token_sums(ref):
        out = []
        for i in range(tokens // 128):
            rs = slice(i * 128, (i + 1) * 128)
            part = p_s[rs, 0:128] * ref[rs, 0:128]
            for j in range(1, width // 128):
                js = slice(j * 128, (j + 1) * 128)
                part = part + p_s[rs, js] * ref[rs, js]
            out.append(jnp.sum(jnp.transpose(part), axis=0, keepdims=True))
        return out

    mine[...] = jnp.concatenate(
        token_sums(pa) + token_sums(pb)
        + [jnp.sum(sq, axis=0, keepdims=True), jnp.sum(cross, axis=0, keepdims=True)], axis=0)

    def send(k):
        o = lax.rem(me + k, n)
        return pltpu.make_async_remote_copy(
            src_ref=mine, dst_ref=inbox.at[n - 1 - k],
            send_sem=ss, recv_sem=sr,
            device_id={"dp": o}, device_id_type=MESH)

    def all_sent():
        return pltpu.make_async_remote_copy(
            src_ref=inbox, dst_ref=inbox,
            send_sem=ss, recv_sem=sr,
            device_id={"dp": sibling}, device_id_type=MESH)

    for k in range(1, n):
        send(k).start()

    def bent_step(i, _):
        rs = pl.ds(pl.multiple_of(i * STRIP, STRIP), STRIP)
        pa[rs, :] = q_s[rs, :] * pa[rs, :]
        pb[rs, :] = q_s[rs, :] * pb[rs, :]
        return 0

    lax.fori_loop(0, tokens // STRIP, bent_step, 0, unroll=4)

    def sent_line(i, _):
        o = (i * wide + y) * 2 + core

        def sent(up):
            pltpu.make_async_remote_copy(
                src_ref=slab(o), dst_ref=slab(o), send_sem=zs.at[0 if up else 1, o], recv_sem=zr.at[0, o],
                device_id={"dp": me + stride if up else me - stride}, device_id_type=MESH).wait_send()

        @pl.when((i <= z) & more)
        def _():
            sent(True)

        @pl.when((i >= z) & less)
        def _():
            sent(False)

        if wide == 2:
            over(o).wait_send()
        return 0

    lax.fori_loop(0, line, sent_line, 0)
    beside_all().wait_send()
    all_sent().wait_recv()

    tot = mine[...]
    for o in range(n - 1):
        tot = tot + inbox[o]
    sq = 0.2 * jnp.sum(tot[2 * spans:2 * spans + 1], keepdims=True)
    cross = math.sqrt(0.2) * jnp.sum(tot[2 * spans + 1:], keepdims=True)
    rms = jnp.sqrt(sq / COUNT)
    scale = 1.0 / jnp.maximum(1.0, rms)
    bind = jnp.where(rms > 1.0, 1.0 / (rms * rms * rms), 0.0)
    alpha = (-0.01 * 0.1 * math.sqrt(20.0)) * scale
    beta = (0.01 * 0.2) * cross * bind / COUNT
    scores = alpha * tot[0:spans] + beta * tot[spans:2 * spans]
    span = lax.broadcasted_iota(jnp.int32, (spans, 128), 0)
    scores = jnp.sum(jnp.where(span == me * rows // 128, scores, 0.0), axis=0, keepdims=True)
    lane = lax.broadcasted_iota(jnp.int32, (128, 128), 0) - lax.rem(me * rows, 128)
    at = lax.broadcasted_iota(jnp.int32, (128, 128), 1)
    column = jnp.transpose(jnp.broadcast_to(scores, (128, 128)))
    score_out[...] = jnp.sum(jnp.where(lane == at, column, 0.0), axis=0, keepdims=True)
    alpha = jnp.broadcast_to(alpha, (STRIP, width))
    beta = jnp.broadcast_to(beta, (STRIP, width))

    def last_step(i, _):
        rs = pl.ds(pl.multiple_of(i * STRIP, STRIP), STRIP)
        bent_out[rs, :] = (alpha * pa[rs, :] + beta * pb[rs, :]).astype(jnp.bfloat16)
        return 0

    lax.fori_loop(0, tokens // STRIP, last_step, 0, unroll=4)
    all_sent().wait_send()


def last_kernel(tok, bent, adj, sc, theta_hbm, score, theta, out_sem):
    step = D // LAST
    parts = [pl.ds(i * step, step) for i in range(LAST)]
    outs = [pltpu.make_async_copy(theta.at[p, :], theta_hbm.at[p, :], out_sem.at[i]) for i, p in enumerate(parts)]
    for i, p in enumerate(parts):
        theta[p, :] = 0.999 * adj[p, :] + dot_rows(tok[:, p], bent[...])
        outs[i].start()
    score[...] = sc[:, :score.shape[1]]
    for copy in outs:
        copy.wait()


def shards(n, wide, x, cotangent, token_weight, weight, moment_one, moment_two, adjoint):
    rows = x.shape[0]
    tokens = n * rows
    width = weight.shape[1]
    pieces = 4 if n <= 16 else 1
    f32, bf16 = jnp.float32, jnp.bfloat16
    vm = pl.BlockSpec(memory_space=pltpu.VMEM)
    hbm = pl.BlockSpec(memory_space=pltpu.HBM)
    dma = pltpu.SemaphoreType.DMA
    tok, adj, bent, sc = pl.pallas_call(
        functools.partial(main_kernel, n, wide, pieces),
        out_shape=(
            pltpu.VMEM((tokens, D), bf16),
            pltpu.VMEM((D, width), f32),
            pltpu.VMEM((tokens, width), bf16),
            pltpu.VMEM((1, 128), f32),
        ),
        in_specs=[hbm] * 7,
        out_specs=(vm, vm, vm, vm),
        scratch_shapes=[
            pltpu.VMEM((tokens, width), bf16),
            pltpu.VMEM((1, tokens), f32),
            pltpu.VMEM((D, width), bf16),
            pltpu.VMEM((D, width), bf16),
            pltpu.VMEM((D, width), bf16),
            pltpu.VMEM((tokens, width), f32),
            pltpu.VMEM((tokens, width), f32),
            pltpu.VMEM((tokens, width), f32),
            pltpu.VMEM((tokens, width), bf16),
            pltpu.VMEM((KB, width), f32),
            pltpu.VMEM((KB, width), bf16),
            pltpu.VMEM((KB, width), bf16),
            pltpu.VMEM((tokens, width), f32),
            pltpu.VMEM((tokens, width), f32),
            pltpu.VMEM((tokens // 64 + 2, 128), f32),
            pltpu.VMEM((n - 1, tokens // 64 + 2, 128), f32),
            dma((3,)),
            dma((3, D // KB)),
            dma,
            dma((2, n)),
            dma((pieces, n)),
            dma((n,)),
            dma((n,)),
            dma,
            dma,
            dma,
            dma,
        ],
        compiler_params=pltpu.CompilerParams(
            collective_id=0, has_side_effects=True, vmem_limit_bytes=36 * 2**20
        ),
    )(*(
        pltpu.with_memory_space_constraint(a, pltpu.HBM)
        for a in (x, cotangent, token_weight.reshape(1, tokens), weight, moment_one, moment_two, adjoint)
    ))
    theta, score = pl.pallas_call(
        last_kernel,
        out_shape=(
            jax.ShapeDtypeStruct((D, width), f32),
            jax.ShapeDtypeStruct((1, rows), f32),
        ),
        in_specs=[vm] * 4,
        out_specs=(hbm, vm),
        scratch_shapes=[pltpu.VMEM((D, width), f32), dma((LAST,))],
        compiler_params=pltpu.CompilerParams(vmem_limit_bytes=36 * 2**20),
    )(tok, bent, adj, sc)
    return theta, score.reshape(rows)


def solution(mesh):
    n = mesh.shape["dp"]
    wide = 2 if mesh.shape["group"] == 2 else 1
    in_specs = (
        P(("group", "dp"), None),
        P("group", "dp"),
        P("group"),
        P(None, "dp"),
        P(None, "dp"),
        P(None, "dp"),
        P(None, "dp"),
    )
    out_specs = (P("group", "dp"), P(("group", "dp")))
    return jax.shard_map(
        functools.partial(shards, n, wide), mesh=mesh,
        in_specs=in_specs, out_specs=out_specs, check_vma=False)
```
